32 devices in a mesh: band: 8 (over z, y), chan: 4 (over x, core).
Axes of the slice: x: 2, y: 2, z: 4, core: 2. Of those that a mesh axis runs over, the one named last changes fastest.
Arguments:
- spectra: bfloat16 [2, 2, 16384, 64], P(None, None, 'chan', 'band')
- window_flags: int32 [2, 128], replicated, may hold values 0 or 1
- pair_tiles: int32 [4, 8, 2], P('chan'), may hold values from 0 to 127, as said below
- owners: int32 [4, 8, 1], P('chan'), may hold values from 0 to 7; in each aligned block of 8 rows (0 to 7, 8 to 15, ..., all dimensions but the last counted through in order) at most 2 rows name the same one
- stacks: float32 [4, 16, 512, 128], P('chan', 'band'), may hold values from -3 to 3
Outputs:
- new_stacks: float32 [4, 16, 512, 128], P('chan', 'band')
The draws below stay inside these ranges and needn't reach their ends.
Inputs may be any that keep to these rules, and one draw needn't show every extreme that they name: `pair_tiles`: entry 0 is a tile of the pair's own quarter q (q * 32 to q * 32 + 31) and entry 1 = entry 0 + d: either 0 <= d <= 7, with d even where entry 1 lies in the quarter above, or -7 <= d < 0 with entry 1 in the quarter below and d odd. No two pair tiles of the whole cable join the same two tiles. Every quarter has a pair with d = 7, and every quarter but the first one with d = -7. `owners`: no owner holds more than 2 pair tiles of one quarter; some owner holds exactly 2.
All inputs are finite; a program needn't handle non-finite values.
Results may differ from the reference program's by a relative error of at most 0.0039.
Values may be sent and summed in bfloat16 or wider, within the bound.
No kernel may reach another device: no remote copies, remote signals or barrier semaphores. Data moves between devices by JAX's collectives and lax.ppermute only.
A program may use at most 64 MiB of HBM per device.

```python
import math
import jax
import jax.numpy as jnp
import numpy as np
from jax import lax

TILE = 128
MAXOFF = 7
LAGS = 512
CAP = 2
W = 2
F_DEV = 8
QUARTERS = 4
CH = 16384
CH_TILES = 128
TQ = 32
NF = 64
PAIRS = 8
SLOTS = 16
N_BAND = 8


def draw_spectra(key, part):
    keys = jax.random.split(key, 3)
    shape = (W, 2, CH, NF)
    channel_level = jnp.exp(jax.random.uniform(keys[2], (W, 1, CH, 1)) * math.log(10.0))
    bin_level = jnp.exp(jax.random.uniform(keys[1], (1, 1, 1, NF)) * math.log(10.0))
    values = jax.random.normal(keys[0], shape) * bin_level * channel_level
    return values.astype(jnp.float32).astype(jnp.bfloat16)


def draw_pair_tiles(key, part):
    span = 2 * MAXOFF + 1
    count = TQ * span
    index = jnp.arange(count, dtype=jnp.int32)
    collected = []
    for quarter in range(QUARTERS):
        lowest = quarter * TQ
        source = lowest + index // span
        offset = index % span - MAXOFF
        target = source + offset
        inside = (target >= 0) & (target < CH_TILES)
        upward = (offset >= 0) & ((target < lowest + TQ) | (offset % 2 == 0))
        downward = (offset < 0) & (target < lowest) & (-offset % 2 == 1)
        valid = inside & (upward | downward)
        score = jax.random.permutation(jax.random.fold_in(key, quarter), count).astype(jnp.int32) + 2
        score = jnp.where((source == lowest) & (offset == -MAXOFF), 0, score)
        score = jnp.where((source == lowest) & (offset == MAXOFF), 1, score)
        score = jnp.where(valid, score, score + 4 * count)
        order = jnp.argsort(score, stable=True)[:PAIRS]
        collected.append(jnp.stack([source[order], target[order]], axis=-1))
    return jnp.stack(collected).astype(jnp.int32)


def touch_ends(values, rng, least, top_value):
    shape = values.shape
    spot = [jax.random.randint(jax.random.fold_in(rng, axis), (), 0, shape[axis]) for axis in range(len(shape))]
    values = values.at[tuple(spot)].set(least)
    longest = shape.index(max(shape))
    spot[longest] = (spot[longest] + 1) % shape[longest]
    return values.at[tuple(spot)].set(top_value)


def levels(stream_key, extent, cuts, least, top_value):
    def one(dim, parts):
        steps = jax.random.uniform(jax.random.fold_in(jax.random.fold_in(stream_key, 6), dim), (parts,), jnp.float32, least / len(cuts), top_value / len(cuts))
        return jnp.repeat(jnp.exp(steps), extent[dim] // parts).reshape((-1,) + (1,) * (len(extent) - dim - 1))

    factor_of = one(*cuts[0])
    for cut in cuts[1:]:
        factor_of = factor_of * one(*cut)
    return factor_of


def shared_out(key, own, number, rows, number_of, top, bound, lean):
    ranking = jax.random.permutation(key, number_of)
    packed, usual = portions_of(number_of, rows * top, bound, lean, True), portions_of(number_of, rows * top, bound, lean, False)
    places = jnp.arange(number_of)

    def named(tallies, rotation):
        used = int((tallies > 0).sum())
        fixed = max(1, used // 4)
        moved = fixed + (places - fixed + rotation * (used - fixed)) % max(1, number_of - fixed)
        return jnp.zeros((number_of,), jnp.int32).at[ranking[jnp.where(places < fixed, places, moved)]].set(jnp.asarray(tallies, jnp.int32))

    tallies = jnp.where(number % 4 == 0, named(packed, number // 4), named(usual, number - number // 4 - 1))
    mixed = jax.random.permutation(jax.random.fold_in(own, 3), number_of)
    donor, taker = mixed[0:number_of // 2 * 2:2], mixed[1:number_of // 2 * 2:2]
    margin = jnp.minimum(tallies[donor] - 1, bound - tallies[taker]) // 2
    margin = jnp.where((donor == ranking[0]) | (taker == ranking[0]) | (tallies[taker] == 0), 0, jnp.maximum(margin, 0))
    moved = jax.random.randint(jax.random.fold_in(own, 4), (number_of // 2,), 0, 1 << 20) % (margin + 1)
    tallies = tallies.at[donor].add(-moved).at[taker].add(moved)
    members = jnp.searchsorted(jnp.cumsum(tallies), jnp.arange(rows * top), side="right").astype(jnp.int32)
    listing = members.reshape(top, rows).T
    listing = listing[jax.random.permutation(jax.random.fold_in(own, 1), rows)]
    rotation = jax.random.randint(jax.random.fold_in(own, 2), (rows, 1), 0, top)
    return jnp.take_along_axis(listing, (jnp.arange(top)[None, :] + rotation) % top, axis=1)


def portions_of(number_of, total, reach, slope, full):
    loads = [(1 << 20) // math.isqrt(standing ** slope) + 1 for standing in range(1, number_of + 1)]
    largest = reach if full else min(reach, max(-(-total // number_of), total * loads[0] // sum(loads)))
    least = 1 if total - largest >= number_of - 1 else 0
    holding, rest = [largest] + [least] * (number_of - 1), total - largest - least * (number_of - 1)
    while rest > 0:
        movable = [i for i in range(1, number_of) if holding[i] < largest] or [i for i in range(1, number_of) if holding[i] < reach]
        mass, remaining = sum([loads[i] for i in movable]), rest
        for i in movable:
            extra = min(reach - holding[i], max(1, remaining * loads[i] // mass), rest)
            holding[i] = holding[i] + extra
            rest = rest - extra
    return np.array(holding)


def gaussian(stream_key, dims, deviation, most, cuts=(), kind=jnp.bfloat16):
    values = deviation * jax.random.normal(stream_key, dims, jnp.float32)
    if cuts:
        values = values * levels(stream_key, dims, cuts, -0.22, 0.18)
    return jnp.clip(values, -most, most).astype(kind)


def setup_inputs(seed: int = 0) -> dict:
    arg_keys = jax.random.split(jax.random.key(seed), 6)
    spectra = draw_spectra(jax.random.fold_in(arg_keys[5], 71), 0)
    window_flags = touch_ends((jax.random.randint(arg_keys[1], (W, CH_TILES), 0, 4) < 3).astype(jnp.int32), jax.random.fold_in(arg_keys[1], 1), 0, 1)
    pair_tiles = draw_pair_tiles(jax.random.fold_in(arg_keys[5], 71), 0)
    owners_keys = jax.random.split(jax.random.fold_in(arg_keys[3], 1), QUARTERS * PAIRS // PAIRS)
    owners_turns = jax.random.permutation(jax.random.fold_in(arg_keys[3], 3), QUARTERS * PAIRS // PAIRS)
    owners = jax.vmap(lambda own, number: shared_out(jax.random.fold_in(arg_keys[3], 2), own, number, PAIRS, N_BAND, 1, CAP, 2))(owners_keys, owners_turns).reshape((QUARTERS, PAIRS, 1))
    stacks = gaussian(arg_keys[4], (QUARTERS, SLOTS, LAGS, TILE), 0.5, 3.0, ((0, 4), (1, 8)), jnp.float32)
    return {"spectra": spectra, "window_flags": window_flags, "pair_tiles": pair_tiles, "owners": owners, "stacks": stacks}


STABILITY_FLOOR = 1e-05

def lag_table(first_bin, bin_count, total_bins):
    frequency = first_bin + lax.iota(jnp.int32, bin_count)
    lag_shift = lax.iota(jnp.int32, LAGS) - LAGS // 2
    phase_index = jnp.mod(lag_shift[:, None] * frequency[None, :], total_bins)
    angles = phase_index.astype(jnp.float32) * (2.0 * math.pi / total_bins)
    amplitude = 1.0 / math.sqrt(total_bins)
    return jnp.concatenate([jnp.cos(angles) * amplitude, -jnp.sin(angles) * amplitude], axis=1).astype(jnp.bfloat16)

def whiten_window(spectrum, tile_validity_flags):
    values = spectrum.astype(jnp.float32)
    energy = values[0] * values[0] + values[1] * values[1]
    block_list = energy.reshape(CH, N_BAND, F_DEV)
    level = jnp.sqrt(lax.optimization_barrier(jnp.mean(block_list, axis=-1)) + STABILITY_FLOOR)
    level = jnp.repeat(level, F_DEV, axis=1)
    gate = jnp.repeat(tile_validity_flags.astype(jnp.float32), TILE)
    return (values / level[None] * gate[None, :, None]).astype(jnp.bfloat16)

def pair_lags(left_tiles, right_tiles, divisor, lag_weights):
    left_real = left_tiles[:, 0].astype(jnp.float32)
    left_imag = left_tiles[:, 1].astype(jnp.float32)
    right_real = right_tiles[:, 0].astype(jnp.float32)
    right_imag = right_tiles[:, 1].astype(jnp.float32)
    real_part = lax.optimization_barrier(jnp.sum(left_real * right_real + left_imag * right_imag, axis=0))
    imaginary_component = lax.optimization_barrier(jnp.sum(left_real * right_imag - left_imag * right_real, axis=0))
    spectrum = (jnp.concatenate([real_part, imaginary_component], axis=-1) / divisor).astype(jnp.bfloat16)
    return jnp.dot(lag_weights.astype(jnp.float32), spectrum.astype(jnp.float32).T, precision=lax.Precision.HIGHEST)

def reference(spectra, window_flags, pair_tiles, owners, stacks):

    def whiten_item(item):
        return whiten_window(item[0], item[1])
    whitened = lax.map(whiten_item, (spectra, window_flags))
    lag_weights = lag_table(0, NF, NF)
    result = stacks
    position = lax.iota(jnp.int32, PAIRS)
    for quarter in range(QUARTERS):
        pair_list = pair_tiles[quarter]
        owner_ids = owners[quarter, :, 0]

        def one_pair(entry):
            source = entry[0]
            target = entry[1]
            left_tiles = lax.dynamic_slice_in_dim(whitened, source * TILE, TILE, 2)
            right_tiles = lax.dynamic_slice_in_dim(whitened, target * TILE, TILE, 2)
            together = jnp.sum(window_flags[:, source] * window_flags[:, target])
            divisor = jnp.maximum(together, 1).astype(jnp.float32)
            return pair_lags(left_tiles, right_tiles, divisor, lag_weights)
        every_lag_value = lax.map(one_pair, pair_list)
        earlier = (owner_ids[:, None] == owner_ids[None, :]) & (position[None, :] < position[:, None])
        slot_rank = lax.optimization_barrier(jnp.sum(earlier.astype(jnp.int32), axis=1))
        slot_index = owner_ids * CAP + slot_rank
        result = result.at[quarter, slot_index].add(every_lag_value)
    return result
```

```python
import functools
import math

import jax
import jax.numpy as jnp
from jax import lax
from jax.experimental import pallas as pl
from jax.experimental.pallas import tpu as pltpu
from jax.sharding import PartitionSpec as P

TILE = 128
MAXOFF = 7
LAGS = 512
CAP = 2


STABILITY_FLOOR = 1e-05


def lag_weights(bin_count, band_size):
    total_bins = bin_count * band_size
    shape = (LAGS, 2 * total_bins)
    column = lax.broadcasted_iota(jnp.int32, shape, 1)
    lag_shift = lax.broadcasted_iota(jnp.int32, shape, 0) - LAGS // 2
    block, within = column // (2 * bin_count), column % (2 * bin_count)
    part, frequency = within // bin_count, block * bin_count + within % bin_count
    phase_index = jnp.mod(lag_shift * frequency, total_bins)
    angles = phase_index.astype(jnp.float32) * (2.0 * math.pi / total_bins)
    amplitude = 1.0 / math.sqrt(total_bins)
    return jnp.where(part == 0, jnp.cos(angles) * amplitude, -jnp.sin(angles) * amplitude).astype(
        jnp.bfloat16
    )


def halos(bins_first, quarter, quarters):
    length = bins_first.shape[3]
    width = MAXOFF * TILE
    first = lax.slice_in_dim(bins_first, 0, width, axis=3)
    last = lax.slice_in_dim(bins_first, length - width, length, axis=3)
    even = quarter % 2 == 0
    near_pairs = [(i, i ^ 1) for i in range(quarters)]
    far_pairs = [(i, (i + 1 if i % 2 else i - 1) % quarters) for i in range(quarters)]
    near = lax.ppermute(jnp.where(even, last, first), "chan", near_pairs)
    far = lax.ppermute(jnp.where(even, first, last), "chan", far_pairs)
    return near, far


def cross_kernel(pairs, owners, flags, own, near, far, out, held):
    windows, bins = own.shape[0], own.shape[2]
    tiles_here = own.shape[3] // TILE
    quarter = lax.axis_index("chan")
    even = lax.rem(quarter, 2) == 0
    base = quarter * tiles_here

    def clear(o, carry):
        held[o] = 0
        return carry

    lax.fori_loop(0, held.shape[0], clear, 0)
    out[...] = jnp.zeros_like(out)

    def tile_of(ref, index):
        start = pl.multiple_of(index * TILE, TILE)
        return ref[:, :, :, pl.ds(start, TILE)].astype(jnp.float32)

    def whiten(values, tile):
        energy = values[:, 0] * values[:, 0] + values[:, 1] * values[:, 1]
        level = jnp.sqrt(jnp.mean(energy, axis=1, keepdims=True) + STABILITY_FLOOR)
        rows = []
        for w in range(windows):
            gate = flags[w, tile].astype(jnp.float32)
            rows.append((values[w] / level[w][None] * gate).astype(jnp.bfloat16).astype(jnp.float32))
        return rows

    def one_pair(p, carry):
        source, target, owner = pairs[0, p], pairs[1, p], owners[0, p]
        here = target - base
        below, above = here < 0, here >= tiles_here
        end = MAXOFF - 1
        below_at = jnp.clip(here + MAXOFF, 0, end)
        above_at = jnp.clip(here - tiles_here, 0, end)
        beside_near = jnp.where(even, above, below)
        beside_far = jnp.where(even, below, above)
        right = tile_of(own, jnp.clip(here, 0, tiles_here - 1))
        right = jnp.where(beside_near, tile_of(near, jnp.where(even, above_at, below_at)), right)
        right = jnp.where(beside_far, tile_of(far, jnp.where(even, below_at, above_at)), right)
        left = whiten(tile_of(own, source - base), source)
        right = whiten(right, target)
        real = imag = None
        together = 0
        for w in range(windows):
            together = together + flags[w, source] * flags[w, target]
            re = left[w][0] * right[w][0] + left[w][1] * right[w][1]
            im = left[w][0] * right[w][1] - left[w][1] * right[w][0]
            real = re if real is None else real + re
            imag = im if imag is None else imag + im
        divisor = jnp.maximum(together, 1).astype(jnp.float32)
        rank = held[owner]
        held[owner] = rank + 1
        spectrum = jnp.concatenate([real, imag], axis=0) / divisor
        out[owner * CAP + rank] = spectrum.astype(jnp.bfloat16)
        return carry

    count = pairs.shape[1]
    lax.fori_loop(0, count, one_pair, 0, unroll=count <= 8)


def in_vmem(array):
    return pltpu.with_memory_space_constraint(array, pltpu.VMEM)


def cross_table(bins_first, near, far, window_flags, pair_list, owner_ids, band_size):
    bins = bins_first.shape[2]
    smem = pl.BlockSpec(memory_space=pltpu.SMEM)
    vmem = pl.BlockSpec(memory_space=pltpu.VMEM)
    return pl.pallas_call(
        cross_kernel,
        out_shape=pltpu.VMEM((band_size * CAP, 2 * bins, TILE), jnp.bfloat16),
        in_specs=[smem, smem, smem, vmem, vmem, vmem],
        out_specs=vmem,
        scratch_shapes=[pltpu.SMEM((band_size,), jnp.int32)],
        name="cross",
    )(pair_list, owner_ids, window_flags, bins_first, in_vmem(near), in_vmem(far))


def stack_kernel(weights, arrived, stacks, out):
    columns = arrived.shape[0] * arrived.shape[2]
    for s in range(arrived.shape[1]):
        spectrum = arrived[:, s].reshape(columns, TILE)
        added = jnp.dot(weights[...], spectrum, preferred_element_type=jnp.float32)
        out[s] = stacks[s] + added


def stack_lags(weights, arrived, stacks):
    vmem = pl.BlockSpec(memory_space=pltpu.VMEM)
    return pl.pallas_call(
        stack_kernel,
        out_shape=jax.ShapeDtypeStruct(stacks.shape, stacks.dtype),
        in_specs=[vmem, vmem, vmem],
        out_specs=vmem,
        name="stack",
    )(in_vmem(weights), in_vmem(arrived), stacks)


def body(spectra, window_flags, pair_tiles, owners, stacks):
    quarter = lax.axis_index("chan")
    band_size, quarters = lax.axis_size("band"), lax.axis_size("chan")
    bins = spectra.shape[3]
    bins_first = jnp.transpose(spectra, (0, 1, 3, 2))
    near, far = halos(bins_first, quarter, quarters)
    table = cross_table(bins_first, near, far, window_flags, pair_tiles[0].T, owners[0].T, band_size)
    arrived = lax.all_to_all(
        table.reshape(band_size, CAP, 2 * bins, TILE), "band", split_axis=0, concat_axis=0, tiled=True
    )
    weights = lag_weights(bins, band_size)
    return stack_lags(weights, arrived, stacks[0])[None]


def solution(mesh):
    in_specs = (
        P(None, None, "chan", "band"),
        P(),
        P("chan", None, None),
        P("chan", None, None),
        P("chan", "band", None, None),
    )
    out_specs = P("chan", "band", None, None)
    return jax.shard_map(body, mesh=mesh, in_specs=in_specs, out_specs=out_specs, check_vma=False)
```

```python
import functools
import math

import jax
import jax.numpy as jnp
from jax import lax
from jax.experimental import pallas as pl
from jax.experimental.pallas import tpu as pltpu
from jax.sharding import PartitionSpec as P

TILE = 128
MAXOFF = 7
LAGS = 512
CAP = 2
KERNEL_VMEM = 16 * 2**20


STABILITY_FLOOR = 1e-05


def lag_weights(bin_count, band_size, band):
    total_bins = bin_count * band_size
    shape = (LAGS, 2 * total_bins)
    column = lax.broadcasted_iota(jnp.int32, shape, 1)
    lag_shift = lax.broadcasted_iota(jnp.int32, shape, 0) - LAGS // 2
    block, within = column // (2 * bin_count), column % (2 * bin_count)
    part, frequency = within // bin_count, (block ^ band) * bin_count + within % bin_count
    phase_index = jnp.mod(lag_shift * frequency, total_bins)
    angles = phase_index.astype(jnp.float32) * (2.0 * math.pi / total_bins)
    amplitude = 1.0 / math.sqrt(total_bins)
    return jnp.where(part == 0, jnp.cos(angles) * amplitude, -jnp.sin(angles) * amplitude).astype(
        jnp.bfloat16
    )


def halos(bins_first, quarter, quarters):
    length = bins_first.shape[3]
    width = MAXOFF * TILE
    first = lax.slice_in_dim(bins_first, 0, width, axis=3)
    last = lax.slice_in_dim(bins_first, length - width, length, axis=3)
    even = quarter % 2 == 0
    near_pairs = [(i, i ^ 1) for i in range(quarters)]
    far_pairs = [(i, (i + 1 if i % 2 else i - 1) % quarters) for i in range(quarters)]
    near = lax.ppermute(jnp.where(even, last, first), "chan", near_pairs)
    far = lax.ppermute(jnp.where(even, first, last), "chan", far_pairs)
    return near, far


def cross_kernel(pairs, owners, flags, own, near, far, out, held):
    windows, bins = own.shape[0], own.shape[2]
    tiles_here = own.shape[3] // TILE
    quarter, band = lax.axis_index("chan"), lax.axis_index("band")
    even = lax.rem(quarter, 2) == 0
    base = quarter * tiles_here

    def clear(o, carry):
        held[o] = 0
        return carry

    lax.fori_loop(0, held.shape[0], clear, 0)
    out[...] = jnp.zeros_like(out)

    def tile_of(ref, index):
        start = pl.multiple_of(index * TILE, TILE)
        return ref[:, :, :, pl.ds(start, TILE)].astype(jnp.float32)

    def whiten(values, tile):
        energy = values[:, 0] * values[:, 0] + values[:, 1] * values[:, 1]
        level = jnp.sqrt(jnp.mean(energy, axis=1, keepdims=True) + STABILITY_FLOOR)
        rows = []
        for w in range(windows):
            gate = flags[w, tile].astype(jnp.float32)
            rows.append((values[w] / level[w][None] * gate).astype(jnp.bfloat16).astype(jnp.float32))
        return rows

    def one_pair(p, carry):
        source, target, owner = pairs[0, p], pairs[1, p], owners[0, p]
        here = target - base
        below, above = here < 0, here >= tiles_here
        end = MAXOFF - 1
        below_at = jnp.clip(here + MAXOFF, 0, end)
        above_at = jnp.clip(here - tiles_here, 0, end)
        beside_near = jnp.where(even, above, below)
        beside_far = jnp.where(even, below, above)
        right = tile_of(own, jnp.clip(here, 0, tiles_here - 1))
        right = jnp.where(beside_near, tile_of(near, jnp.where(even, above_at, below_at)), right)
        right = jnp.where(beside_far, tile_of(far, jnp.where(even, below_at, above_at)), right)
        left = whiten(tile_of(own, source - base), source)
        right = whiten(right, target)
        real = imag = None
        together = 0
        for w in range(windows):
            together = together + flags[w, source] * flags[w, target]
            re = left[w][0] * right[w][0] + left[w][1] * right[w][1]
            im = left[w][0] * right[w][1] - left[w][1] * right[w][0]
            real = re if real is None else real + re
            imag = im if imag is None else imag + im
        divisor = jnp.maximum(together, 1).astype(jnp.float32)
        rank = held[owner]
        held[owner] = rank + 1
        spectrum = jnp.concatenate([real, imag], axis=0) / divisor
        out[(owner ^ band) * CAP + rank] = spectrum.astype(jnp.bfloat16)
        return carry

    count = pairs.shape[1]
    lax.fori_loop(0, count, one_pair, 0, unroll=count <= 8)


def in_vmem(array):
    return pltpu.with_memory_space_constraint(array, pltpu.VMEM)


def in_smem(array):
    return pltpu.with_memory_space_constraint(array, pltpu.SMEM)


def cross_table(bins_first, near, far, window_flags, pair_list, owner_ids, band_size):
    bins = bins_first.shape[2]
    smem = pl.BlockSpec(memory_space=pltpu.SMEM)
    vmem = pl.BlockSpec(memory_space=pltpu.VMEM)
    return pl.pallas_call(
        cross_kernel,
        out_shape=pltpu.VMEM((band_size * CAP, 2 * bins, TILE), jnp.bfloat16),
        in_specs=[smem, smem, smem, vmem, vmem, vmem],
        out_specs=vmem,
        scratch_shapes=[pltpu.SMEM((band_size,), jnp.int32)],
        compiler_params=pltpu.CompilerParams(vmem_limit_bytes=KERNEL_VMEM),
        name="cross",
    )(in_smem(pair_list), in_smem(owner_ids), in_smem(window_flags), in_vmem(bins_first), in_vmem(near), in_vmem(far))


def exchange(table, band_size):
    held = table[None]
    for stage in range(band_size.bit_length() - 1):
        pairs = [(i, i ^ (1 << stage)) for i in range(band_size)]
        split = held.reshape(held.shape[0], held.shape[1] // 2, 2, *held.shape[2:])
        came = lax.ppermute(split[:, :, 1], "band", pairs)
        held = jnp.concatenate([split[:, :, 0], came], axis=0)
    return held[:, 0]


def stack_kernel(weights, arrived, stacks, out, sums, sems):
    columns = arrived.shape[0] * arrived.shape[2]
    lags = sums.shape[1]
    parts = sems.shape[1]
    rows = lags // parts
    copies = []
    for s in range(arrived.shape[1]):
        spectrum = arrived[:, s].reshape(columns, TILE)
        for part in range(parts):
            here = pl.ds(part * rows, rows)
            added = jnp.dot(weights[here, :], spectrum, preferred_element_type=jnp.float32)
            sums[s, here, :] = stacks[s, here, :] + added
            copy = pltpu.make_async_copy(sums.at[s, here, :], out.at[s, here, :], sems.at[s, part])
            copy.start()
            copies.append(copy)
    for copy in copies:
        copy.wait()


def stack_lags(weights, arrived, stacks):
    vmem = pl.BlockSpec(memory_space=pltpu.VMEM)
    return pl.pallas_call(
        stack_kernel,
        out_shape=jax.ShapeDtypeStruct(stacks.shape, stacks.dtype),
        in_specs=[vmem, vmem, vmem],
        out_specs=pl.BlockSpec(memory_space=pl.ANY),
        scratch_shapes=[
            pltpu.VMEM(stacks.shape, stacks.dtype),
            pltpu.SemaphoreType.DMA((stacks.shape[0], 2)),
        ],
        compiler_params=pltpu.CompilerParams(vmem_limit_bytes=KERNEL_VMEM),
        name="stack",
    )(in_vmem(weights), in_vmem(arrived), in_vmem(stacks))


def body(spectra, window_flags, pair_tiles, owners, stacks):
    quarter = lax.axis_index("chan")
    band_size, quarters = lax.axis_size("band"), lax.axis_size("chan")
    bins = spectra.shape[3]
    bins_first = jnp.transpose(spectra, (0, 1, 3, 2))
    near, far = halos(bins_first, quarter, quarters)
    table = cross_table(bins_first, near, far, window_flags, pair_tiles[0].T, owners[0].T, band_size)
    arrived = exchange(table.reshape(band_size, CAP, 2 * bins, TILE), band_size)
    weights = lag_weights(bins, band_size, lax.axis_index("band"))
    return stack_lags(weights, arrived, stacks[0])[None]


def solution(mesh):
    in_specs = (
        P(None, None, "chan", "band"),
        P(),
        P("chan", None, None),
        P("chan", None, None),
        P("chan", "band", None, None),
    )
    out_specs = P("chan", "band", None, None)
    return jax.shard_map(body, mesh=mesh, in_specs=in_specs, out_specs=out_specs, check_vma=False)
```

```python
import math

import jax
import jax.numpy as jnp
from jax import lax
from jax.experimental import pallas as pl
from jax.experimental.pallas import tpu as pltpu
from jax.sharding import PartitionSpec as P


TILE = 128
MAXOFF = 7
LAGS = 512
CAP = 2
WIDTH = 2
KERNEL_VMEM = 16 * 2**20


STABILITY_FLOOR = 1e-05


def lag_weights(bin_count, band_size, band):
    total_bins = bin_count * band_size
    shape = (LAGS, 2 * total_bins)
    column = lax.broadcasted_iota(jnp.int32, shape, 1)
    lag_shift = lax.broadcasted_iota(jnp.int32, shape, 0) - LAGS // 2
    block, within = column // (2 * bin_count), column % (2 * bin_count)
    part, frequency = within // bin_count, (block ^ band) * bin_count + within % bin_count
    phase_index = jnp.mod(lag_shift * frequency, total_bins)
    angles = phase_index.astype(jnp.float32) * (2.0 * math.pi / total_bins)
    amplitude = 1.0 / math.sqrt(total_bins)
    return jnp.where(part == 0, jnp.cos(angles) * amplitude, -jnp.sin(angles) * amplitude).astype(
        jnp.bfloat16
    )


def halos(bins_first, quarter, quarters):
    length = bins_first.shape[3]
    width = MAXOFF * TILE
    first = lax.slice_in_dim(bins_first, 0, width, axis=3)
    last = lax.slice_in_dim(bins_first, length - width, length, axis=3)
    even = quarter % 2 == 0
    near_pairs = [(i, i ^ 1) for i in range(quarters)]
    far_pairs = [(i, (i + 1 if i % 2 else i - 1) % quarters) for i in range(quarters)]
    near = lax.ppermute(jnp.where(even, last, first), "chan", near_pairs)
    far = lax.ppermute(jnp.where(even, first, last), "chan", far_pairs)
    return near, far


def tile_of(ref, index):
    start = pl.multiple_of(index * TILE, TILE)
    return ref[:, :, :, pl.ds(start, TILE)].astype(jnp.float32)


def level_of(values):
    energy = values[0] * values[0] + values[1] * values[1]
    return jnp.sqrt(jnp.mean(energy, axis=0, keepdims=True) + STABILITY_FLOOR)[None]


def rounded(values):
    return values.astype(jnp.bfloat16).astype(jnp.float32)


def spectrum_of(left, right):
    real = imag = None
    for a, b in zip(left, right):
        re, im = a[0] * b[0] + a[1] * b[1], a[0] * b[1] - a[1] * b[0]
        real, imag = (re, im) if real is None else (real + re, imag + im)
    return jnp.concatenate([real, imag], axis=0).astype(jnp.bfloat16)


def prepare_kernel(pairs, owners, flags, own, info, left, table, held):
    windows = own.shape[0]
    tiles_here = own.shape[3] // TILE
    quarter, band = lax.axis_index("chan"), lax.axis_index("band")
    even = lax.rem(quarter, 2) == 0
    base = quarter * tiles_here
    row = lax.broadcasted_iota(jnp.int32, info.shape, 0)
    lane = lax.broadcasted_iota(jnp.int32, info.shape, 1)

    def clear(o, carry):
        held[o] = 0
        return carry

    lax.fori_loop(0, held.shape[0], clear, 0)
    table[...] = jnp.zeros_like(table)

    def one_pair(p, notes):
        source, target, owner = pairs[0, p], pairs[1, p], owners[0, p]
        here = target - base
        below, above = here < 0, here >= tiles_here
        side = jnp.where(jnp.where(even, above, below), 1, jnp.where(below | above, 2, 0))
        beside = jnp.clip(jnp.where(below, here + MAXOFF, here - tiles_here), 0, MAXOFF - 1)
        rank = held[owner]
        held[owner] = rank + 1
        slot = (owner ^ band) * CAP + rank
        together = 0
        for w in range(windows):
            together = together + flags[w, source] * flags[w, target]
        divisor = jnp.maximum(together, 1).astype(jnp.float32)
        values = tile_of(own, source - base)
        other = tile_of(own, jnp.clip(here, 0, tiles_here - 1))
        lefts, rights = [], []
        for w in range(windows):
            gate = flags[w, source].astype(jnp.float32)
            tile = rounded(values[w] / level_of(values[w]) * gate)
            tile = tile * flags[w, target].astype(jnp.float32) / divisor
            left[p, w] = tile
            lefts.append(tile)
            rights.append(rounded(other[w] / level_of(other[w])))
        spectrum = spectrum_of(lefts, rights)
        table[slot] = jnp.where(side == 0, spectrum, jnp.zeros_like(spectrum))
        for i, value in enumerate((side, beside, slot)):
            notes = jnp.where((row == i) & (lane == p), value, notes)
        return notes

    count = pairs.shape[1]
    info[...] = lax.fori_loop(
        0, count, one_pair, jnp.zeros(info.shape, jnp.int32), unroll=count <= 8
    )


def finish_kernel(info, left, near, far, table, out, notes, sem):
    copy = pltpu.make_async_copy(info, notes, sem)
    copy.start()
    out[...] = table[...]
    copy.wait()

    def one_pair(p, carry):
        side, beside, slot = notes[0, p], notes[1, p], notes[2, p]
        values = jnp.where(side == 1, tile_of(near, beside), tile_of(far, beside))
        windows = values.shape[0]
        rights = [rounded(values[w] / level_of(values[w])) for w in range(windows)]
        spectrum = spectrum_of([left[p, w] for w in range(windows)], rights)
        out[slot] = jnp.where(side == 0, table[slot], spectrum)
        return carry

    count = left.shape[0]
    lax.fori_loop(0, count, one_pair, 0, unroll=count <= 8)


def in_vmem(array):
    return pltpu.with_memory_space_constraint(array, pltpu.VMEM)


SMEM = pl.BlockSpec(memory_space=pltpu.SMEM)
VMEM = pl.BlockSpec(memory_space=pltpu.VMEM)
PARAMS = pltpu.CompilerParams(vmem_limit_bytes=KERNEL_VMEM)


def prepare(bins_first, window_flags, pair_list, owner_ids, band_size):
    windows, _, bins, _ = bins_first.shape
    count = pair_list.shape[1]
    return pl.pallas_call(
        prepare_kernel,
        out_shape=[
            pltpu.VMEM((8, pl.cdiv(count, 128) * 128), jnp.int32),
            pltpu.VMEM((count, windows, 2, bins, TILE), jnp.float32),
            pltpu.VMEM((band_size * CAP, 2 * bins, TILE), jnp.bfloat16),
        ],
        in_specs=[SMEM, SMEM, SMEM, VMEM],
        out_specs=[VMEM, VMEM, VMEM],
        scratch_shapes=[pltpu.SMEM((band_size,), jnp.int32)],
        compiler_params=PARAMS,
        name="prepare",
    )(pair_list, owner_ids, window_flags, in_vmem(bins_first))


def finish(info, left, table, near, far):
    return pl.pallas_call(
        finish_kernel,
        out_shape=pltpu.VMEM(table.shape, table.dtype),
        in_specs=[VMEM] * 5,
        out_specs=VMEM,
        scratch_shapes=[pltpu.SMEM(info.shape, jnp.int32), pltpu.SemaphoreType.DMA],
        compiler_params=PARAMS,
        name="finish",
    )(*map(in_vmem, (info, left, near, far, table)))


def exchange(table, band_size, quarters):
    bits = band_size.bit_length() - 1
    starts = range(0, bits, WIDTH)
    turns = len(starts) - len(starts) % 2 if quarters % 2 == 0 else 0
    held = table[None]
    for stage, low in enumerate(starts):
        ways = 1 << min(WIDTH, bits - low)
        split = held.reshape(held.shape[0], held.shape[1] // ways, ways, *held.shape[2:])
        parts = []
        for way in range(ways):
            flip = (way << low) * quarters + (1 if stage < turns else 0)
            pairs = [(i, i ^ flip) for i in range(band_size * quarters)]
            part = split[:, :, way]
            parts.append(lax.ppermute(part, ("band", "chan"), pairs) if flip else part)
        held = jnp.concatenate(parts, axis=0)
    return held[:, 0]


def stack_kernel(weights, arrived, stacks, out, sums, sems):
    columns = arrived.shape[0] * arrived.shape[2]
    lags = sums.shape[1]
    parts = sems.shape[1]
    rows = lags // parts
    copies = []
    for s in range(arrived.shape[1]):
        spectrum = arrived[:, s].reshape(columns, TILE)
        for part in range(parts):
            here = pl.ds(part * rows, rows)
            added = jnp.dot(weights[here, :], spectrum, preferred_element_type=jnp.float32)
            sums[s, here, :] = stacks[s, here, :] + added
            copy = pltpu.make_async_copy(sums.at[s, here, :], out.at[s, here, :], sems.at[s, part])
            copy.start()
            copies.append(copy)
    for copy in copies:
        copy.wait()


def stack_lags(weights, arrived, stacks):
    return pl.pallas_call(
        stack_kernel,
        out_shape=jax.ShapeDtypeStruct(stacks.shape, stacks.dtype),
        in_specs=[VMEM, VMEM, VMEM],
        out_specs=pl.BlockSpec(memory_space=pl.ANY),
        scratch_shapes=[
            pltpu.VMEM(stacks.shape, stacks.dtype),
            pltpu.SemaphoreType.DMA((stacks.shape[0], 2)),
        ],
        compiler_params=PARAMS,
        name="stack",
    )(in_vmem(weights), in_vmem(arrived), in_vmem(stacks))


def body(spectra, window_flags, pair_tiles, owners, stacks):
    quarter = lax.axis_index("chan")
    band_size, quarters = lax.axis_size("band"), lax.axis_size("chan")
    bins = spectra.shape[3]
    bins_first = jnp.transpose(spectra, (0, 1, 3, 2))
    near, far = halos(bins_first, quarter, quarters)
    info, left, table = prepare(
        bins_first, window_flags, pair_tiles[0].T, owners[0].T, band_size
    )
    table = finish(info, left, table, near, far)
    arrived = exchange(table.reshape(band_size, CAP, 2 * bins, TILE), band_size, quarters)
    weights = lag_weights(bins, band_size, lax.axis_index("band"))
    return stack_lags(weights, arrived, stacks[0])[None]


def solution(mesh):
    in_specs = (
        P(None, None, "chan", "band"),
        P(),
        P("chan", None, None),
        P("chan", None, None),
        P("chan", "band", None, None),
    )
    out_specs = P("chan", "band", None, None)
    return jax.shard_map(body, mesh=mesh, in_specs=in_specs, out_specs=out_specs, check_vma=False)
```

```python
import math

import jax
import jax.numpy as jnp
from jax import lax
from jax.experimental import pallas as pl
from jax.experimental.pallas import tpu as pltpu
from jax.sharding import PartitionSpec as P


TILE = 128
MAXOFF = 7
LAGS = 512
CAP = 2
WIDTH = 2
KERNEL_VMEM = 16 * 2**20


STABILITY_FLOOR = 1e-05


def lag_weights(bin_count, band_size, band):
    total_bins = bin_count * band_size
    shape = (LAGS, 2 * total_bins)
    column = lax.broadcasted_iota(jnp.int32, shape, 1)
    lag_shift = lax.broadcasted_iota(jnp.int32, shape, 0) - LAGS // 2
    block, within = column // (2 * bin_count), column % (2 * bin_count)
    part, frequency = within // bin_count, (block ^ band) * bin_count + within % bin_count
    phase_index = jnp.mod(lag_shift * frequency, total_bins)
    angles = phase_index.astype(jnp.float32) * (2.0 * math.pi / total_bins)
    amplitude = 1.0 / math.sqrt(total_bins)
    return jnp.where(part == 0, jnp.cos(angles) * amplitude, -jnp.sin(angles) * amplitude).astype(
        jnp.bfloat16
    )


def halos(bins_first, quarter, quarters):
    length = bins_first.shape[3]
    width = MAXOFF * TILE
    first = lax.slice_in_dim(bins_first, 0, width, axis=3)
    last = lax.slice_in_dim(bins_first, length - width, length, axis=3)
    even = quarter % 2 == 0
    near_pairs = [(i, i ^ 1) for i in range(quarters)]
    far_pairs = [(i, (i + 1 if i % 2 else i - 1) % quarters) for i in range(quarters)]
    near = lax.ppermute(jnp.where(even, last, first), "chan", near_pairs)
    far = lax.ppermute(jnp.where(even, first, last), "chan", far_pairs)
    return near, far


def tile_of(ref, index):
    start = pl.multiple_of(index * TILE, TILE)
    return ref[:, :, :, pl.ds(start, TILE)].astype(jnp.float32)


def level_of(values):
    energy = values[0] * values[0] + values[1] * values[1]
    return jnp.sqrt(jnp.mean(energy, axis=0, keepdims=True) + STABILITY_FLOOR)[None]


def rounded(values):
    return values.astype(jnp.bfloat16).astype(jnp.float32)


def spectrum_of(left, right):
    real = imag = None
    for a, b in zip(left, right):
        re, im = a[0] * b[0] + a[1] * b[1], a[0] * b[1] - a[1] * b[0]
        real, imag = (re, im) if real is None else (real + re, imag + im)
    return jnp.concatenate([real, imag], axis=0).astype(jnp.bfloat16)


def prepare_kernel(pairs, owners, flags, own, info, left, table, held):
    windows = own.shape[0]
    tiles_here = own.shape[3] // TILE
    quarter, band = lax.axis_index("chan"), lax.axis_index("band")
    even = lax.rem(quarter, 2) == 0
    base = quarter * tiles_here

    def clear(o, carry):
        held[o] = 0
        return carry

    lax.fori_loop(0, held.shape[0], clear, 0)
    table[...] = jnp.zeros_like(table)

    def one_pair(p, carry):
        source, target, owner = pairs[0, p], pairs[1, p], owners[0, p]
        here = target - base
        below, above = here < 0, here >= tiles_here
        side = jnp.where(jnp.where(even, above, below), 1, jnp.where(below | above, 2, 0))
        beside = jnp.clip(jnp.where(below, here + MAXOFF, here - tiles_here), 0, MAXOFF - 1)
        rank = held[owner]
        held[owner] = rank + 1
        slot = (owner ^ band) * CAP + rank
        together = 0
        for w in range(windows):
            together = together + flags[w, source] * flags[w, target]
        divisor = jnp.maximum(together, 1).astype(jnp.float32)
        values = tile_of(own, source - base)
        other = tile_of(own, jnp.clip(here, 0, tiles_here - 1))
        lefts, rights = [], []
        for w in range(windows):
            gate = flags[w, source].astype(jnp.float32)
            tile = rounded(values[w] / level_of(values[w]) * gate)
            tile = tile * flags[w, target].astype(jnp.float32) / divisor
            left[p, w] = tile
            lefts.append(tile)
            rights.append(rounded(other[w] / level_of(other[w])))
        spectrum = spectrum_of(lefts, rights)
        table[slot] = jnp.where(side == 0, spectrum, jnp.zeros_like(spectrum))
        info[p] = jnp.full(info.shape[1:], (slot * MAXOFF + beside) * 3 + side)
        return carry

    count = pairs.shape[1]
    lax.fori_loop(0, count, one_pair, 0, unroll=count <= 8)


def finish_kernel(info, left, near, far, table, out):
    out[...] = table[...]

    def one_pair(p, carry):
        note = info[p][0, 0]
        side, beside, slot = note % 3, note // 3 % MAXOFF, note // (3 * MAXOFF)
        values = jnp.where(side == 1, tile_of(near, beside), tile_of(far, beside))
        windows = values.shape[0]
        rights = [rounded(values[w] / level_of(values[w])) for w in range(windows)]
        spectrum = spectrum_of([left[p, w] for w in range(windows)], rights)
        out[slot] = jnp.where(side == 0, table[slot], spectrum)
        return carry

    count = left.shape[0]
    lax.fori_loop(0, count, one_pair, 0, unroll=count <= 8)


def in_vmem(array):
    return pltpu.with_memory_space_constraint(array, pltpu.VMEM)


SMEM = pl.BlockSpec(memory_space=pltpu.SMEM)
VMEM = pl.BlockSpec(memory_space=pltpu.VMEM)
PARAMS = pltpu.CompilerParams(vmem_limit_bytes=KERNEL_VMEM)


def prepare(bins_first, window_flags, pair_list, owner_ids, band_size):
    windows, _, bins, _ = bins_first.shape
    count = pair_list.shape[1]
    return pl.pallas_call(
        prepare_kernel,
        out_shape=[
            pltpu.VMEM((count, 8, TILE), jnp.int32),
            pltpu.VMEM((count, windows, 2, bins, TILE), jnp.float32),
            pltpu.VMEM((band_size * CAP, 2 * bins, TILE), jnp.bfloat16),
        ],
        in_specs=[SMEM, SMEM, SMEM, VMEM],
        out_specs=[VMEM, VMEM, VMEM],
        scratch_shapes=[pltpu.SMEM((band_size,), jnp.int32)],
        compiler_params=PARAMS,
        name="prepare",
    )(pair_list, owner_ids, window_flags, in_vmem(bins_first))


def finish(info, left, table, near, far):
    return pl.pallas_call(
        finish_kernel,
        out_shape=pltpu.VMEM(table.shape, table.dtype),
        in_specs=[VMEM] * 5,
        out_specs=VMEM,
        compiler_params=PARAMS,
        name="finish",
    )(*map(in_vmem, (info, left, near, far, table)))


def exchange(table, band_size, quarters):
    bits = band_size.bit_length() - 1
    starts = range(0, bits, WIDTH)
    turns = len(starts) - len(starts) % 2 if quarters % 2 == 0 else 0
    held = table[None]
    for stage, low in enumerate(starts):
        ways = 1 << min(WIDTH, bits - low)
        split = held.reshape(held.shape[0], held.shape[1] // ways, ways, *held.shape[2:])
        parts = []
        for way in range(ways):
            flip = (way << low) * quarters + (1 if stage < turns else 0)
            pairs = [(i, i ^ flip) for i in range(band_size * quarters)]
            part = split[:, :, way]
            parts.append(lax.ppermute(part, ("band", "chan"), pairs) if flip else part)
        held = jnp.concatenate(parts, axis=0)
    return held[:, 0]


def stack_kernel(weights, arrived, stacks, out, sums, sems):
    columns = arrived.shape[0] * arrived.shape[2]
    lags = sums.shape[1]
    parts = sems.shape[1]
    rows = lags // parts
    copies = []
    for s in range(arrived.shape[1]):
        spectrum = arrived[:, s].reshape(columns, TILE)
        for part in range(parts):
            here = pl.ds(part * rows, rows)
            added = jnp.dot(weights[here, :], spectrum, preferred_element_type=jnp.float32)
            sums[s, here, :] = stacks[s, here, :] + added
            copy = pltpu.make_async_copy(sums.at[s, here, :], out.at[s, here, :], sems.at[s, part])
            copy.start()
            copies.append(copy)
    for copy in copies:
        copy.wait()


def stack_lags(weights, arrived, stacks):
    return pl.pallas_call(
        stack_kernel,
        out_shape=jax.ShapeDtypeStruct(stacks.shape, stacks.dtype),
        in_specs=[VMEM, VMEM, VMEM],
        out_specs=pl.BlockSpec(memory_space=pl.ANY),
        scratch_shapes=[
            pltpu.VMEM(stacks.shape, stacks.dtype),
            pltpu.SemaphoreType.DMA((stacks.shape[0], 2)),
        ],
        compiler_params=PARAMS,
        name="stack",
    )(in_vmem(weights), in_vmem(arrived), in_vmem(stacks))


def body(spectra, window_flags, pair_tiles, owners, stacks):
    quarter = lax.axis_index("chan")
    band_size, quarters = lax.axis_size("band"), lax.axis_size("chan")
    bins = spectra.shape[3]
    bins_first = jnp.transpose(spectra, (0, 1, 3, 2))
    near, far = halos(bins_first, quarter, quarters)
    info, left, table = prepare(
        bins_first, window_flags, pair_tiles[0].T, owners[0].T, band_size
    )
    table = finish(info, left, table, near, far)
    arrived = exchange(table.reshape(band_size, CAP, 2 * bins, TILE), band_size, quarters)
    weights = lag_weights(bins, band_size, lax.axis_index("band"))
    return stack_lags(weights, arrived, stacks[0])[None]


def solution(mesh):
    in_specs = (
        P(None, None, "chan", "band"),
        P(),
        P("chan", None, None),
        P("chan", None, None),
        P("chan", "band", None, None),
    )
    out_specs = P("chan", "band", None, None)
    return jax.shard_map(body, mesh=mesh, in_specs=in_specs, out_specs=out_specs, check_vma=False)
```

```python
import math

import jax
import jax.numpy as jnp
from jax import lax
from jax.experimental import pallas as pl
from jax.experimental.pallas import tpu as pltpu
from jax.sharding import PartitionSpec as P


TILE = 128
MAXOFF = 7
LAGS = 512
CAP = 2
KERNEL_VMEM = 16 * 2**20


STABILITY_FLOOR = 1e-05


def lag_weights(bin_count, band_size, band):
    total_bins = bin_count * band_size
    shape = (LAGS, 2 * total_bins)
    column = lax.broadcasted_iota(jnp.int32, shape, 1)
    lag_shift = lax.broadcasted_iota(jnp.int32, shape, 0) - LAGS // 2
    block, within = column // (2 * bin_count), column % (2 * bin_count)
    part, frequency = within // bin_count, (block ^ band) * bin_count + within % bin_count
    phase_index = jnp.mod(lag_shift * frequency, total_bins)
    angles = phase_index.astype(jnp.float32) * (2.0 * math.pi / total_bins)
    amplitude = 1.0 / math.sqrt(total_bins)
    return jnp.where(part == 0, jnp.cos(angles) * amplitude, -jnp.sin(angles) * amplitude).astype(
        jnp.bfloat16
    )


def halos(bins_first, quarter, quarters):
    length = bins_first.shape[3]
    width = MAXOFF * TILE
    first = lax.slice_in_dim(bins_first, 0, width, axis=3)
    last = lax.slice_in_dim(bins_first, length - width, length, axis=3)
    even = quarter % 2 == 0
    near_pairs = [(i, i ^ 1) for i in range(quarters)]
    far_pairs = [(i, (i + 1 if i % 2 else i - 1) % quarters) for i in range(quarters)]
    near = lax.ppermute(jnp.where(even, last, first), "chan", near_pairs)
    far = lax.ppermute(jnp.where(even, first, last), "chan", far_pairs)
    return near, far


def tile_of(ref, index):
    start = pl.multiple_of(index * TILE, TILE)
    return ref[:, :, :, pl.ds(start, TILE)].astype(jnp.float32)


def level_of(values):
    energy = values[0] * values[0] + values[1] * values[1]
    return jnp.sqrt(jnp.mean(energy, axis=0, keepdims=True) + STABILITY_FLOOR)[None]


def rounded(values):
    return values.astype(jnp.bfloat16).astype(jnp.float32)


def spectrum_of(left, right):
    real = imag = None
    for a, b in zip(left, right):
        re, im = a[0] * b[0] + a[1] * b[1], a[0] * b[1] - a[1] * b[0]
        real, imag = (re, im) if real is None else (real + re, imag + im)
    return jnp.concatenate([real, imag], axis=0).astype(jnp.bfloat16)


def prepare_kernel(pairs, owners, flags, own, info, left, table, held):
    windows = own.shape[0]
    tiles_here = own.shape[3] // TILE
    quarter, band = lax.axis_index("chan"), lax.axis_index("band")
    even = lax.rem(quarter, 2) == 0
    base = quarter * tiles_here

    def clear(o, carry):
        held[o] = 0
        return carry

    lax.fori_loop(0, held.shape[0], clear, 0)
    table[...] = jnp.zeros_like(table)

    def one_pair(p, carry):
        source, target, owner = pairs[0, p], pairs[1, p], owners[0, p]
        here = target - base
        below, above = here < 0, here >= tiles_here
        side = jnp.where(jnp.where(even, above, below), 1, jnp.where(below | above, 2, 0))
        beside = jnp.clip(jnp.where(below, here + MAXOFF, here - tiles_here), 0, MAXOFF - 1)
        rank = held[owner]
        held[owner] = rank + 1
        slot = (owner ^ band) * CAP + rank
        together = 0
        for w in range(windows):
            together = together + flags[w, source] * flags[w, target]
        divisor = jnp.maximum(together, 1).astype(jnp.float32)
        values = tile_of(own, source - base)
        other = tile_of(own, jnp.clip(here, 0, tiles_here - 1))
        lefts, rights = [], []
        for w in range(windows):
            gate = flags[w, source].astype(jnp.float32)
            tile = rounded(values[w] / level_of(values[w]) * gate)
            tile = tile * flags[w, target].astype(jnp.float32) / divisor
            left[p, w] = tile
            lefts.append(tile)
            rights.append(rounded(other[w] / level_of(other[w])))
        spectrum = spectrum_of(lefts, rights)
        table[slot] = jnp.where(side == 0, spectrum, jnp.zeros_like(spectrum))
        info[p] = jnp.full(info.shape[1:], (slot * MAXOFF + beside) * 3 + side)
        return carry

    count = pairs.shape[1]
    lax.fori_loop(0, count, one_pair, 0, unroll=count <= 8)


def finish_kernel(info, left, near, far, table, out):
    out[...] = table[...]

    def one_pair(p, carry):
        note = info[p][0, 0]
        side, beside, slot = note % 3, note // 3 % MAXOFF, note // (3 * MAXOFF)
        values = jnp.where(side == 1, tile_of(near, beside), tile_of(far, beside))
        windows = values.shape[0]
        rights = [rounded(values[w] / level_of(values[w])) for w in range(windows)]
        spectrum = spectrum_of([left[p, w] for w in range(windows)], rights)
        out[slot] = jnp.where(side == 0, table[slot], spectrum)
        return carry

    count = left.shape[0]
    lax.fori_loop(0, count, one_pair, 0, unroll=count <= 8)


def in_hbm(array):
    return pltpu.with_memory_space_constraint(array, pltpu.HBM)


def in_vmem(array):
    return pltpu.with_memory_space_constraint(array, pltpu.VMEM)


SMEM = pl.BlockSpec(memory_space=pltpu.SMEM)
VMEM = pl.BlockSpec(memory_space=pltpu.VMEM)
PARAMS = pltpu.CompilerParams(vmem_limit_bytes=KERNEL_VMEM)


def prepare(bins_first, window_flags, pair_list, owner_ids, band_size):
    windows, _, bins, _ = bins_first.shape
    count = pair_list.shape[1]
    return pl.pallas_call(
        prepare_kernel,
        out_shape=[
            pltpu.VMEM((count, 8, TILE), jnp.int32),
            pltpu.VMEM((count, windows, 2, bins, TILE), jnp.float32),
            pltpu.VMEM((band_size * CAP, 2 * bins, TILE), jnp.bfloat16),
        ],
        in_specs=[SMEM, SMEM, SMEM, VMEM],
        out_specs=[VMEM, VMEM, VMEM],
        scratch_shapes=[pltpu.SMEM((band_size,), jnp.int32)],
        compiler_params=PARAMS,
        name="prepare",
    )(*map(in_hbm, (pair_list, owner_ids, window_flags)), in_vmem(bins_first))


def finish(info, left, table, near, far):
    return pl.pallas_call(
        finish_kernel,
        out_shape=pltpu.VMEM(table.shape, table.dtype),
        in_specs=[VMEM] * 5,
        out_specs=VMEM,
        compiler_params=PARAMS,
        name="finish",
    )(*map(in_vmem, (info, left, near, far, table)))


def stages_of(band_size):
    bits = band_size.bit_length() - 1
    lows = range(bits - 2, -1, -2) if bits % 2 == 0 else (bits - 1, *range(bits - 3, -1, -2))
    return [(low, 1 if low == bits - 1 else 2) for low in lows]


def turns_of(stages, quarters):
    return len(stages) - len(stages) % 2 if quarters % 2 == 0 else 0


def exchange(table, band_size, quarters):
    stages = stages_of(band_size)
    turns = turns_of(stages, quarters)
    held = table[None]
    for stage, (low, width) in enumerate(stages):
        ways = 1 << width
        split = held.reshape(held.shape[0], ways, 1 << low, *held.shape[2:])
        parts = []
        for way in range(ways):
            flip = (way << low) * quarters + (1 if stage < turns else 0)
            pairs = [(i, i ^ flip) for i in range(band_size * quarters)]
            part = split[:, way]
            parts.append(lax.ppermute(part, ("band", "chan"), pairs) if flip else part)
        held = jnp.stack(parts, axis=1).reshape(held.shape[0] * ways, 1 << low, *held.shape[2:])
    return held[:, 0]


def stack_kernel(weights, arrived, stacks, out, sums, sems):
    columns = arrived.shape[0] * arrived.shape[2]
    lags = sums.shape[1]
    parts = sems.shape[1]
    rows = lags // parts
    copies = []
    for s in range(arrived.shape[1]):
        spectrum = arrived[:, s].reshape(columns, TILE)
        for part in range(parts):
            here = pl.ds(part * rows, rows)
            added = jnp.dot(weights[here, :], spectrum, preferred_element_type=jnp.float32)
            sums[s, here, :] = stacks[s, here, :] + added
            copy = pltpu.make_async_copy(sums.at[s, here, :], out.at[s, here, :], sems.at[s, part])
            copy.start()
            copies.append(copy)
    for copy in copies:
        copy.wait()


def stack_lags(weights, arrived, stacks):
    return pl.pallas_call(
        stack_kernel,
        out_shape=jax.ShapeDtypeStruct(stacks.shape, stacks.dtype),
        in_specs=[VMEM, VMEM, VMEM],
        out_specs=pl.BlockSpec(memory_space=pl.ANY),
        scratch_shapes=[
            pltpu.VMEM(stacks.shape, stacks.dtype),
            pltpu.SemaphoreType.DMA((stacks.shape[0], 2)),
        ],
        compiler_params=PARAMS,
        name="stack",
    )(in_vmem(weights), in_vmem(arrived), in_vmem(stacks))


def body(spectra, window_flags, pair_tiles, owners, stacks):
    quarter = lax.axis_index("chan")
    band_size, quarters = lax.axis_size("band"), lax.axis_size("chan")
    bins = spectra.shape[3]
    bins_first = jnp.transpose(spectra, (0, 1, 3, 2))
    near, far = halos(bins_first, quarter, quarters)
    info, left, table = prepare(
        bins_first, window_flags, pair_tiles[0].T, owners[0].T, band_size
    )
    table = finish(info, left, table, near, far)
    arrived = exchange(table.reshape(band_size, CAP, 2 * bins, TILE), band_size, quarters)
    weights = lag_weights(bins, band_size, lax.axis_index("band"))
    return stack_lags(weights, arrived, stacks[0])[None]


def solution(mesh):
    in_specs = (
        P(None, None, "chan", "band"),
        P(),
        P("chan", None, None),
        P("chan", None, None),
        P("chan", "band", None, None),
    )
    out_specs = P("chan", "band", None, None)
    return jax.shard_map(body, mesh=mesh, in_specs=in_specs, out_specs=out_specs, check_vma=False)
```

```python
import math

import jax
import jax.numpy as jnp
from jax import lax
from jax.experimental import pallas as pl
from jax.experimental.pallas import tpu as pltpu
from jax.sharding import PartitionSpec as P


TILE = 128
MAXOFF = 7
LAGS = 512
CAP = 2
KERNEL_VMEM = 16 * 2**20


STABILITY_FLOOR = 1e-05


def lag_weights(bin_count, band_size, band):
    total_bins = bin_count * band_size
    shape = (LAGS, 2 * total_bins)
    column = lax.broadcasted_iota(jnp.int32, shape, 1)
    lag_shift = lax.broadcasted_iota(jnp.int32, shape, 0) - LAGS // 2
    block, within = column // (2 * bin_count), column % (2 * bin_count)
    part, frequency = within // bin_count, (block ^ band) * bin_count + within % bin_count
    phase_index = jnp.mod(lag_shift * frequency, total_bins)
    angles = phase_index.astype(jnp.float32) * (2.0 * math.pi / total_bins)
    amplitude = 1.0 / math.sqrt(total_bins)
    return jnp.where(part == 0, jnp.cos(angles) * amplitude, -jnp.sin(angles) * amplitude).astype(
        jnp.bfloat16
    )


def halos(bins_first, quarter, quarters):
    length = bins_first.shape[3]
    width = MAXOFF * TILE
    first = lax.slice_in_dim(bins_first, 0, width, axis=3)
    last = lax.slice_in_dim(bins_first, length - width, length, axis=3)
    even = quarter % 2 == 0
    near_pairs = [(i, i ^ 1) for i in range(quarters)]
    far_pairs = [(i, (i + 1 if i % 2 else i - 1) % quarters) for i in range(quarters)]
    near = lax.ppermute(jnp.where(even, last, first), "chan", near_pairs)
    far = lax.ppermute(jnp.where(even, first, last), "chan", far_pairs)
    return near, far


def tile_of(ref, index):
    start = pl.multiple_of(index * TILE, TILE)
    return ref[:, :, :, pl.ds(start, TILE)].astype(jnp.float32)


def level_of(values):
    energy = values[0] * values[0] + values[1] * values[1]
    return jnp.sqrt(jnp.mean(energy, axis=0, keepdims=True) + STABILITY_FLOOR)[None]


def rounded(values):
    return values.astype(jnp.bfloat16).astype(jnp.float32)


def spectrum_of(left, right):
    real = imag = None
    for a, b in zip(left, right):
        re, im = a[0] * b[0] + a[1] * b[1], a[0] * b[1] - a[1] * b[0]
        real, imag = (re, im) if real is None else (real + re, imag + im)
    return jnp.concatenate([real, imag], axis=0).astype(jnp.bfloat16)


def prepare_kernel(pairs, owners, flags, own, info, left, table, held):
    windows = own.shape[0]
    tiles_here = own.shape[3] // TILE
    quarter, band = lax.axis_index("chan"), lax.axis_index("band")
    even = lax.rem(quarter, 2) == 0
    base = quarter * tiles_here

    def clear(o, carry):
        held[o] = 0
        return carry

    lax.fori_loop(0, held.shape[0], clear, 0)
    table[...] = jnp.zeros_like(table)

    def one_pair(p, carry):
        source, target, owner = pairs[0, p], pairs[1, p], owners[0, p]
        here = target - base
        below, above = here < 0, here >= tiles_here
        side = jnp.where(jnp.where(even, above, below), 1, jnp.where(below | above, 2, 0))
        beside = jnp.clip(jnp.where(below, here + MAXOFF, here - tiles_here), 0, MAXOFF - 1)
        rank = held[owner]
        held[owner] = rank + 1
        slot = (owner ^ band) * CAP + rank
        together = 0
        for w in range(windows):
            together = together + flags[w, source] * flags[w, target]
        divisor = jnp.maximum(together, 1).astype(jnp.float32)
        values = tile_of(own, source - base)
        other = tile_of(own, jnp.clip(here, 0, tiles_here - 1))
        lefts, rights = [], []
        for w in range(windows):
            gate = flags[w, source].astype(jnp.float32)
            tile = rounded(values[w] / level_of(values[w]) * gate)
            tile = tile * flags[w, target].astype(jnp.float32) / divisor
            left[p, w] = tile
            lefts.append(tile)
            rights.append(rounded(other[w] / level_of(other[w])))
        spectrum = spectrum_of(lefts, rights)
        table[slot] = jnp.where(side == 0, spectrum, jnp.zeros_like(spectrum))
        info[p] = jnp.full(info.shape[1:], (slot * MAXOFF + beside) * 3 + side)
        return carry

    count = pairs.shape[1]
    lax.fori_loop(0, count, one_pair, 0, unroll=count <= 8)


def finish_kernel(info, left, near, far, table, out):
    out[...] = table[...]

    def one_pair(p, carry):
        note = info[p][0, 0]
        side, beside, slot = note % 3, note // 3 % MAXOFF, note // (3 * MAXOFF)
        values = jnp.where(side == 1, tile_of(near, beside), tile_of(far, beside))
        windows = values.shape[0]
        rights = [rounded(values[w] / level_of(values[w])) for w in range(windows)]
        spectrum = spectrum_of([left[p, w] for w in range(windows)], rights)
        out[slot] = jnp.where(side == 0, table[slot], spectrum)
        return carry

    count = left.shape[0]
    lax.fori_loop(0, count, one_pair, 0, unroll=count <= 8)


def in_hbm(array):
    return pltpu.with_memory_space_constraint(array, pltpu.HBM)


def in_vmem(array):
    return pltpu.with_memory_space_constraint(array, pltpu.VMEM)


SMEM = pl.BlockSpec(memory_space=pltpu.SMEM)
VMEM = pl.BlockSpec(memory_space=pltpu.VMEM)
PARAMS = pltpu.CompilerParams(vmem_limit_bytes=KERNEL_VMEM)


def prepare(bins_first, window_flags, pair_list, owner_ids, band_size):
    windows, _, bins, _ = bins_first.shape
    count = pair_list.shape[1]
    return pl.pallas_call(
        prepare_kernel,
        out_shape=[
            pltpu.VMEM((count, 8, TILE), jnp.int32),
            pltpu.VMEM((count, windows, 2, bins, TILE), jnp.float32),
            pltpu.VMEM((band_size * CAP, 2 * bins, TILE), jnp.bfloat16),
        ],
        in_specs=[SMEM, SMEM, SMEM, VMEM],
        out_specs=[VMEM, VMEM, VMEM],
        scratch_shapes=[pltpu.SMEM((band_size,), jnp.int32)],
        compiler_params=PARAMS,
        name="prepare",
    )(*map(in_hbm, (pair_list, owner_ids, window_flags)), in_vmem(bins_first))


def finish(info, left, table, near, far):
    return pl.pallas_call(
        finish_kernel,
        out_shape=pltpu.VMEM(table.shape, table.dtype),
        in_specs=[VMEM] * 5,
        out_specs=VMEM,
        compiler_params=PARAMS,
        name="finish",
    )(*map(in_vmem, (info, left, near, far, table)))


def stages_of(band_size):
    bits = band_size.bit_length() - 1
    lows = range(bits - 2, -1, -2) if bits % 2 == 0 else (bits - 1, *range(bits - 3, -1, -2))
    return [(low, 1 if low == bits - 1 else 2) for low in lows]


def turns_of(stages, quarters):
    return len(stages) - len(stages) % 2 if quarters % 2 == 0 else 0


def exchange(table, band_size, quarters):
    stages = stages_of(band_size)
    turns = turns_of(stages, quarters)
    held = table[None]
    for stage, (low, width) in enumerate(stages):
        ways = 1 << width
        split = held.reshape(held.shape[0], ways, 1 << low, *held.shape[2:])
        parts = []
        for way in range(ways):
            flip = (way << low) * quarters + (1 if stage < turns else 0)
            pairs = [(i, i ^ flip) for i in range(band_size * quarters)]
            part = split[:, way]
            parts.append(lax.ppermute(part, ("band", "chan"), pairs) if flip else part)
        if low:
            held = jnp.stack(parts, axis=1).reshape(-1, 1 << low, *held.shape[2:])
    return [part[:, 0] for part in parts]


def stack_kernel(weights, stacks, *refs):
    *arrived, out, sums, sems = refs
    columns = weights.shape[1]
    lags = sums.shape[1]
    parts = sems.shape[1]
    rows = lags // parts
    copies = []
    for s in range(stacks.shape[0]):
        spectrum = jnp.stack([part[:, s] for part in arrived], axis=1).reshape(columns, TILE)
        for part in range(parts):
            here = pl.ds(part * rows, rows)
            added = jnp.dot(weights[here, :], spectrum, preferred_element_type=jnp.float32)
            sums[s, here, :] = stacks[s, here, :] + added
            copy = pltpu.make_async_copy(sums.at[s, here, :], out.at[s, here, :], sems.at[s, part])
            copy.start()
            copies.append(copy)
    for copy in copies:
        copy.wait()


def stack_lags(weights, arrived, stacks):
    return pl.pallas_call(
        stack_kernel,
        out_shape=jax.ShapeDtypeStruct(stacks.shape, stacks.dtype),
        in_specs=[VMEM] * (2 + len(arrived)),
        out_specs=pl.BlockSpec(memory_space=pl.ANY),
        scratch_shapes=[
            pltpu.VMEM(stacks.shape, stacks.dtype),
            pltpu.SemaphoreType.DMA((stacks.shape[0], 2)),
        ],
        compiler_params=PARAMS,
        name="stack",
    )(*map(in_vmem, (weights, stacks, *arrived)))


def body(spectra, window_flags, pair_tiles, owners, stacks):
    quarter = lax.axis_index("chan")
    band_size, quarters = lax.axis_size("band"), lax.axis_size("chan")
    bins = spectra.shape[3]
    bins_first = jnp.transpose(spectra, (0, 1, 3, 2))
    near, far = halos(bins_first, quarter, quarters)
    info, left, table = prepare(
        bins_first, window_flags, pair_tiles[0].T, owners[0].T, band_size
    )
    table = finish(info, left, table, near, far)
    arrived = exchange(table.reshape(band_size, CAP, 2 * bins, TILE), band_size, quarters)
    weights = lag_weights(bins, band_size, lax.axis_index("band"))
    return stack_lags(weights, arrived, stacks[0])[None]


def solution(mesh):
    in_specs = (
        P(None, None, "chan", "band"),
        P(),
        P("chan", None, None),
        P("chan", None, None),
        P("chan", "band", None, None),
    )
    out_specs = P("chan", "band", None, None)
    return jax.shard_map(body, mesh=mesh, in_specs=in_specs, out_specs=out_specs, check_vma=False)
```
